32 devices in a mesh: seg: 2 (over y), row: 8 (over z, x), col: 2 (over core).
Axes of the slice: x: 2, y: 2, z: 4, core: 2. Of those that a mesh axis runs over, the one named last changes fastest.
Arguments:
- slices: bfloat16 [4, 4096, 4096], P('col', 'seg', 'row'), may hold values from -1 to 1
Outputs:
- prefixes: bfloat16 [4, 4096, 4096], P('col', 'seg', 'row')
The draws below stay inside these ranges and needn't reach their ends.
All inputs are finite; a program needn't handle non-finite values.
Results may differ from the reference program's by a relative error of at most 0.004.
Values may be sent and summed in bfloat16 or wider, within the bound.
No kernel may reach another device: no remote copies, remote signals or barrier semaphores. Data moves between devices by JAX's collectives and lax.ppermute only.
A program may use at most 128 MiB of HBM per device.

```python
import math
import jax
import jax.numpy as jnp
from jax import lax

ORDER = 4096
SEG_DEV = 2
SEGMENTS = 4
N_COL = 2


def draw_slices(key, part):
    shape = (SEGMENTS, ORDER, ORDER)
    noise = jnp.clip(jax.random.normal(key, shape, jnp.float32), -6.0, 6.0)
    identity = jnp.eye(ORDER, dtype=jnp.float32)
    matrix = (identity[None] + noise / math.sqrt(ORDER)) * 0.70710678
    return matrix.astype(jnp.bfloat16)


def setup_inputs(seed: int = 0) -> dict:
    splits = jax.random.split(jax.random.key(seed), 2)
    return {
        "slices": draw_slices(jax.random.fold_in(splits[1], 71), 0),
    }


def multiply(left_factor, right_factor):
    product = jnp.einsum('gij,gjk->gik', left_factor.astype(jnp.float32), right_factor.astype(jnp.float32), precision=lax.Precision.HIGHEST)
    return product.astype(jnp.bfloat16)

def reference(slices):
    blocks = slices.reshape(N_COL, SEG_DEV, ORDER, ORDER)
    history = [blocks[:, 0]]
    for position in range(1, SEG_DEV):
        history.append(multiply(blocks[:, position], history[-1]))
    running = history[-1]
    distance = 1
    while distance < N_COL:
        product = multiply(running[distance:], running[:-distance])
        running = jnp.concatenate([running[:distance], product], axis=0)
        distance = distance * 2
    local_chain = jnp.stack(history, axis=1)
    factor = math.sqrt(ORDER)
    carried = running[:-1].astype(jnp.float32)
    later = jnp.einsum('gsij,gjk->gsik', local_chain[1:].astype(jnp.float32), carried, precision=lax.Precision.HIGHEST) * factor
    first = local_chain[:1].astype(jnp.float32) * factor
    result = jnp.concatenate([first, later], axis=0).astype(jnp.bfloat16)
    return result.reshape(SEGMENTS, ORDER, ORDER)
```

```python
import math

import jax
import jax.numpy as jnp
from jax import lax
from jax.experimental import pallas as pl
from jax.experimental.pallas import tpu as pltpu
from jax.sharding import PartitionSpec as P


def fast_length(mesh):
    count = mesh.shape["row"]
    line = mesh.devices.reshape(mesh.shape["seg"], count, mesh.shape["col"])[0, :, 0]
    coords = [getattr(d, "coords", None) for d in line]
    if count < 2 or any(c is None for c in coords):
        return 1
    moving = [a for a in range(len(coords[0])) if coords[0][a] != coords[1][a]]
    if len(moving) != 1:
        return 1
    length = 1
    while length < count and all(
        coords[length][a] == coords[0][a] for a in range(len(coords[0])) if a != moving[0]
    ):
        length += 1
    return length if count % length == 0 else 1


def after(value, *others):
    return lax.optimization_barrier((value, *others))[0]


def product_kernel(n_left, n_right, by_half, scale, place, *refs):
    left = refs[:n_left]
    right = refs[n_left : n_left + n_right]
    out, lscr, rscr, acc, lsem, rsem = refs[n_left + n_right :]
    _, segs, subs, cores, _, _ = rscr.shape

    def right_target(y, s, c):
        return rscr.at[s, y, :, c] if by_half else rscr.at[:, y, s, c]

    for i in range(n_left):
        k = place[0, i]
        pltpu.make_async_copy(left[i], lscr.at[k], lsem.at[k]).start()
    for i in range(n_right):
        y, s, c = place[1, i], place[2, i], place[3, i]
        pltpu.make_async_copy(right[i], right_target(y, s, c), rsem.at[y, s, c]).start()
    k = 0
    for y in range(segs):
        for s in range(subs):
            for c in range(cores):
                pltpu.make_async_copy(left[0], lscr.at[k], lsem.at[k]).wait()
                for wanted in range(subs) if by_half and s == 0 else ([] if by_half else [s]):
                    pltpu.make_async_copy(right[0], right_target(y, wanted, c), rsem.at[y, wanted, c]).wait()
                for h in range(2):
                    term = jnp.dot(lscr[k], rscr[h, y, s, c], preferred_element_type=jnp.float32)
                    if k == 0:
                        acc[h] = term
                    elif k < segs * subs * cores - 1:
                        acc[h] += term
                    else:
                        out[h] = ((acc[h] + term) * scale).astype(out.dtype)
                k += 1


def product(left, right, by_half, scale, segs, place):
    q, w = left[0].shape
    n_left, n_right = len(left), len(right)

    def body(place_ref, *refs):
        product_kernel(n_left, n_right, by_half, scale, place_ref, *refs)

    order = n_left * w
    return pl.pallas_call(
        body,
        out_shape=jax.ShapeDtypeStruct((2, q, w), jnp.bfloat16),
        in_specs=[pl.BlockSpec(memory_space=pltpu.SMEM)]
        + [pl.BlockSpec(memory_space=pl.ANY)] * (n_left + n_right),
        out_specs=pl.BlockSpec(memory_space=pltpu.VMEM),
        scratch_shapes=[
            pltpu.VMEM((n_left, q, w), jnp.bfloat16),
            pltpu.VMEM((2, segs, 2, 2, q, w), jnp.bfloat16),
            pltpu.VMEM((2, q, w), jnp.float32),
            pltpu.SemaphoreType.DMA((n_left,)),
            pltpu.SemaphoreType.DMA((segs, 2, 2)),
        ],
        cost_estimate=pl.CostEstimate(
            flops=4 * q * order * w, bytes_accessed=2 * order * (q + 2 * w), transcendentals=0
        ),
        compiler_params=pltpu.CompilerParams(vmem_limit_bytes=40 << 20),
    )(place, *left, *right)


def local(fast, slices):
    segs, rows, _ = (lax.axis_size(a) for a in ("seg", "row", "col"))
    slow = rows // fast
    height, w = slices.shape[1:]
    q = height // 4
    y, r, c = (lax.axis_index(a) for a in ("seg", "row", "col"))
    z, x = r // fast, r % fast
    zl = z % 2
    factor = math.sqrt(segs * height)

    def send(value, axes, pairs, gate=None):
        if gate is not None:
            value = after(value, gate)
        return lax.ppermute(value, axes, pairs)

    def along(value, dz, dx, gate=None):
        pairs = [
            (i, ((i // fast + dz) % slow) * fast + (i % fast + dx) % fast) for i in range(rows)
        ]
        return send(value, "row", pairs, gate)

    def seg_shift(value, dy):
        return send(value, "seg", [(i, (i + dy) % segs) for i in range(segs)])

    def partner(i):
        return ((i // fast) ^ 1) * fast + i % fast

    def plane_swap(value, gate=None):
        return send(value, "row", [(i, partner(i)) for i in range(rows)], gate)

    def core_swap(value):
        return send(value, "col", [(0, 1), (1, 0)])

    def row_half(block, i):
        return lax.dynamic_index_in_dim(block, i, 0, keepdims=False)

    class Left:
        def __init__(self, block):
            self.same, self.other = row_half(block, zl), row_half(block, 1 - zl)
            self.pieces = []

        def over_slow(self, j, gate=None):
            piece = along(self.same if j % 2 == 0 else self.other, j, 0, gate)
            return j, piece

        def over_fast(self, j_piece):
            j, piece = j_piece
            self.pieces.append((j, 0, piece))
            for i in range(1, fast):
                self.pieces.append((j, i, along(piece, 0, i)))

        def places(self):
            return [((z - j) % slow) * fast + (x - i) % fast for j, i, _ in self.pieces]

    class Right:
        def __init__(self, block):
            self.pieces = [(0, 0, 0, block)]

        def places(self):
            return [
                [(y - dy) % segs for dy, _, _, _ in self.pieces],
                [zl ^ s for _, s, _, _ in self.pieces],
                [c ^ k for _, _, k, _ in self.pieces],
            ]

        def near(self, gate=None):
            block = self.pieces[0][-1]
            self.plane = plane_swap(block, gate)
            self.pieces.append((0, 1, 0, self.plane))
            for dy in range(1, segs):
                self.pieces.append((dy, 0, 0, seg_shift(block, dy)))

        def far(self):
            for dy in range(1, segs):
                self.pieces.append((dy, 1, 0, seg_shift(self.plane, dy)))

        def cross(self, dy, s):
            (block,) = [b for p, t, k, b in self.pieces if (p, t, k) == (dy, s, 0)]
            self.pieces.append((dy, s, 1, core_swap(block)))

    def multiply(left, right, by_half, scale):
        table = [left.places()] + right.places()
        width = max(len(t) for t in table)
        zero = jnp.int32(0)
        place = jnp.stack(
            [jnp.stack([jnp.asarray(v, jnp.int32) for v in t] + [zero] * (width - len(t))) for t in table]
        )
        return product(
            [p[-1] for p in left.pieces], [p[-1] for p in right.pieces], by_half, scale, segs, place
        )

    def own_block(right):
        found = {(s, k): row_half(b, zl) for dy, s, k, b in right.pieces if dy == 0}

        def pick(s, k):
            by_core = [jnp.where(c == k, found[(t, 0)], found[(t, 1)]) for t in range(2)]
            return jnp.where(zl == s, by_core[0], by_core[1])

        return jnp.stack([jnp.stack([pick(s, k) for k in range(2)]) for s in range(2)])

    parts = slices.reshape(2, 2, 2, q, w)
    mine = lax.dynamic_index_in_dim(parts, c, 2, keepdims=False)
    theirs = core_swap(lax.dynamic_index_in_dim(parts, 1 - c, 2, keepdims=False))
    right = Right(jnp.where(c == 0, mine[0], theirs[0]))
    lefts = [
        Left(jnp.where(c == 0, mine[1], theirs[1])),
        Left(jnp.where(c == 0, theirs[0], mine[0])),
        Left(jnp.where(c == 0, theirs[1], mine[1])),
    ]
    evens, odds = range(2, slow, 2), range(1, slow, 2)

    left = lefts[0]
    right.near()
    pending = [left.over_slow(j) for j in evens]
    for item in lefts:
        item.over_fast((0, item.same))
    right.cross(0, 0)
    for item in pending:
        left.over_fast(item)
    gate, before = right.plane, None
    for j in odds:
        item = left.over_slow(j, gate)
        if before is None:
            right.far()
            right.cross(0, 1)
            for dy in range(1, segs):
                right.cross(dy, 0)
        else:
            left.over_fast(before)
        gate, before = item[1], item

    rights = []
    for n in range(3):
        following = lefts[n + 1] if n < 2 else None
        if following:
            early = [following.over_slow(j, gate) for j in (*evens, *odds[:1])]
        left.over_fast(before)
        for dy in range(1, segs):
            right.cross(dy, 1)
        carried = multiply(left, right, n == 0, factor if n == 2 else 1.0)
        rights.append(right)
        if not following:
            break
        left, right = following, Right(carried)
        right.near()
        right.cross(0, 0)
        for item in early:
            left.over_fast(item)
        gate, before = right.plane, None
        right.far()
        for j in odds[1:]:
            item = left.over_slow(j, gate)
            if before is None:
                right.cross(0, 1)
                for dy in range(1, segs):
                    right.cross(dy, 0)
            else:
                left.over_fast(before)
            gate, before = item[1], item

    keep, away = row_half(carried, zl), row_half(carried, 1 - zl)
    moved = [
        send(away, ("row", "col"), [(i * 2 + k, partner(i) * 2 + 1) for i in range(rows)])
        for k in range(2)
    ]
    kept = send(keep, "col", [(0, 1)])
    local_rows = jnp.stack([kept, keep])
    far_rows = jnp.stack(moved)
    final = jnp.stack([jnp.where(zl == s, local_rows, far_rows) for s in range(2)])

    def scaled(value):
        return (value.astype(jnp.float32) * factor).astype(jnp.bfloat16)

    head = jnp.where(c == 0, slices[0].reshape(2, 2, q, w), own_block(rights[2]))
    tail = jnp.where(c == 0, scaled(own_block(rights[1])), final)
    return jnp.stack([scaled(head).reshape(height, w), tail.reshape(height, w)], axis=0)


def solution(mesh):
    spec = P("col", "seg", "row")
    fast = fast_length(mesh)

    def body(slices):
        return local(fast, slices)

    return jax.shard_map(body, mesh=mesh, in_specs=(spec,), out_specs=spec, check_vma=False)
```

```python
import functools
import math

import jax
import jax.numpy as jnp
from jax import lax
from jax.experimental import pallas as pl
from jax.experimental.pallas import tpu as pltpu
from jax.sharding import PartitionSpec as P


def fast_length(mesh):
    count = mesh.shape["row"]
    line = mesh.devices.reshape(mesh.shape["seg"], count, mesh.shape["col"])[0, :, 0]
    coords = [getattr(d, "coords", None) for d in line]
    if count < 2 or any(c is None for c in coords):
        return 1
    moving = [a for a in range(len(coords[0])) if coords[0][a] != coords[1][a]]
    if len(moving) != 1:
        return 1
    length = 1
    while length < count and all(
        coords[length][a] == coords[0][a] for a in range(len(coords[0])) if a != moving[0]
    ):
        length += 1
    return length if count % length == 0 else 1


def after(value, *others):
    return lax.optimization_barrier((value, *others))[0]


def product_kernel(n_left, n_right, by_half, earlier, scale, place, *refs):
    left, refs = refs[:n_left], refs[n_left:]
    right, refs = refs[:n_right], refs[n_right:]
    before, refs = refs[:earlier], refs[earlier:]
    *outs, lscr, rscr, acc, lsem, rsem, asem = refs
    halves, _, subs, cores, _, _ = rscr.shape

    def right_copy(i):
        y, s, c = place[1, i], place[2, i], place[3, i]
        target = rscr.at[s, y, :, c] if by_half else rscr.at[0, y, s, c]
        return pltpu.make_async_copy(right[i], target, rsem.at[y, s, c])

    for i in range(n_right):
        pl.when(place[4, i] == 1)(right_copy(i).start)
    for i in range(n_left):
        pltpu.make_async_copy(left[i], lscr.at[i], lsem.at[i]).start()
    copies = [pltpu.make_async_copy(b, acc.at[h], asem.at[h]) for h, b in enumerate(before)]
    for copy in copies:
        copy.start()
    for copy in copies:
        copy.wait()
    if by_half:
        for i in range(n_right):
            pl.when(place[4, i] == 1)(right_copy(i).wait)
    for i in range(n_left):
        k = place[0, i]
        y, s, c = k // (subs * cores), (k // cores) % subs, k % cores
        pltpu.make_async_copy(left[i], lscr.at[i], lsem.at[i]).wait()
        if not by_half:
            pltpu.make_async_copy(right[0], rscr.at[0, y, s, c], rsem.at[y, s, c]).wait()
        for h in range(halves):
            term = jnp.dot(lscr[i], rscr[h, y, s, c], preferred_element_type=jnp.float32)
            if i or earlier:
                term += acc[h]
            if i < n_left - 1:
                acc[h] = term
            else:
                outs[h][...] = (term * scale).astype(outs[h].dtype)


def product(left, right, before, by_half, scale, segs, place, final):
    q, w = left[0].shape
    n_left, n_right = len(left), len(right)
    halves = 2 if by_half else 1

    def body(place_ref, *refs):
        product_kernel(n_left, n_right, by_half, len(before), scale, place_ref, *refs)

    return pl.pallas_call(
        body,
        out_shape=[jax.ShapeDtypeStruct((q, w), jnp.bfloat16 if final else jnp.float32)] * halves,
        in_specs=[pl.BlockSpec(memory_space=pltpu.SMEM)]
        + [pl.BlockSpec(memory_space=pl.ANY)] * (n_left + n_right + len(before)),
        out_specs=[pl.BlockSpec(memory_space=pltpu.VMEM)] * halves,
        scratch_shapes=[
            pltpu.VMEM((n_left, q, w), jnp.bfloat16),
            pltpu.VMEM((halves, segs, 2, 2, q, w), jnp.bfloat16),
            pltpu.VMEM((halves, q, w), jnp.float32),
            pltpu.SemaphoreType.DMA((n_left,)),
            pltpu.SemaphoreType.DMA((segs, 2, 2)),
            pltpu.SemaphoreType.DMA((halves,)),
        ],
        cost_estimate=pl.CostEstimate(
            flops=2 * halves * q * n_left * w * w, bytes_accessed=2 * n_left * w * (q + halves * w), transcendentals=0
        ),
        compiler_params=pltpu.CompilerParams(vmem_limit_bytes=40 << 20),
    )(place, *left, *right, *before)


def local(fast, slices):
    segs, rows, _ = (lax.axis_size(a) for a in ("seg", "row", "col"))
    slow = rows // fast
    height, w = slices.shape[1:]
    q = height // 4
    y, r, c = (lax.axis_index(a) for a in ("seg", "row", "col"))
    z, x = r // fast, r % fast
    zl = z % 2
    factor = math.sqrt(segs * height)

    def send(value, axes, pairs, gate=None):
        if gate is not None:
            value = after(value, gate)
        return lax.ppermute(value, axes, pairs)

    def along(value, dz, dx, gate=None):
        pairs = [
            (i, ((i // fast + dz) % slow) * fast + (i % fast + dx) % fast) for i in range(rows)
        ]
        return send(value, "row", pairs, gate)

    def seg_shift(value, dy, gate=None):
        return send(value, "seg", [(i, (i + dy) % segs) for i in range(segs)], gate)

    def partner(i):
        return ((i // fast) ^ 1) * fast + i % fast

    def plane_swap(value, gate=None):
        return send(value, "row", [(i, partner(i)) for i in range(rows)], gate)

    def core_swap(value):
        return send(value, "col", [(0, 1), (1, 0)])

    def row_half(block, i):
        return lax.dynamic_index_in_dim(block, i, 0, keepdims=False)

    class Left:
        def __init__(self, block):
            self.same, self.other = row_half(block, zl), row_half(block, 1 - zl)
            self.pieces = []

        def over_slow(self, j, gate=None):
            piece = along(self.same if j % 2 == 0 else self.other, j, 0, gate)
            return j, piece

        def over_fast(self, j_piece):
            j, piece = j_piece
            self.pieces.append((j, 0, piece))
            for i in range(1, fast):
                self.pieces.append((j, i, along(piece, 0, i)))

        def places(self):
            return [((z - j) % slow) * fast + (x - i) % fast for j, i, _ in self.pieces]

    class Right:
        def __init__(self, block):
            self.pieces = [(0, 0, 0, block)]

        def places(self):
            return [
                [(y - dy) % segs for dy, _, _, _ in self.pieces],
                [zl ^ s for _, s, _, _ in self.pieces],
                [c ^ k for _, _, k, _ in self.pieces],
            ]

        def add(self, key, block):
            self.pieces.append((*key, block))
            return block

        def block(self, *key):
            return [p[-1] for p in self.pieces if p[:3] == key][0]

        def plane(self, gate=None):
            return self.add((0, 1, 0), plane_swap(self.block(0, 0, 0), gate))

        def segs(self, s, gate=None):
            block = self.block(0, s, 0)
            return [self.add((dy, s, 0), seg_shift(block, dy, gate)) for dy in range(1, segs)]

        def cross(self, s, others=False):
            for dy in range(1, segs) if others else [0]:
                self.add((dy, s, 1), core_swap(self.block(dy, s, 0)))

    def part(left, chosen, right, before, by_half, scale, final):
        places = [left.places()[i] for i in chosen]
        table = [places] + right.places()
        flags = []
        for ry, rs, rc in zip(*table[1:]):
            match = lambda k: (k // 4 == ry) & (k % 2 == rc) & (by_half | (k // 2 % 2 == rs))
            flags.append(functools.reduce(jnp.logical_or, [match(k) for k in places]))
        table.append(flags)
        width = max(len(t) for t in table)
        zero = jnp.int32(0)
        place = jnp.stack(
            [jnp.stack([jnp.asarray(v, jnp.int32) for v in t] + [zero] * (width - len(t))) for t in table]
        )
        return product(
            [left.pieces[i][-1] for i in chosen],
            [p[-1] for p in right.pieces],
            before,
            by_half,
            scale,
            segs,
            place,
            final,
        )

    def own_block(halves):
        found = {
            (t, k): jnp.where(zl == 0, *(right.block(0, t, k) for right in halves))
            for t in range(2)
            for k in range(2)
        }

        def pick(s, k):
            by_core = [jnp.where(c == k, found[(t, 0)], found[(t, 1)]) for t in range(2)]
            return jnp.where(zl == s, by_core[0], by_core[1])

        return jnp.stack([jnp.stack([pick(s, k) for k in range(2)]) for s in range(2)])

    evens, odds = range(2, slow, 2), range(1, slow, 2)

    parts = slices.reshape(2, 2, 2, q, w)
    theirs = [core_swap(jnp.where(c == 0, parts[0, :, 1], parts[0, :, 0]))]
    right = Right(jnp.where(c == 0, parts[0, :, 0], theirs[0]))
    plane = right.plane()
    given = after(parts[1], right.block(0, 0, 0))
    theirs.append(core_swap(jnp.where(c == 0, given[:, 1], given[:, 0])))
    right.segs(0)
    left = Left(jnp.where(c == 0, parts[1, :, 0], theirs[1]))
    coming = [left.over_slow(j) for j in evens]
    left.over_fast((0, left.same))
    theirs = after(theirs, left.same)
    left2 = Left(jnp.where(c == 0, theirs[0], parts[0, :, 1]))
    left3 = Left(jnp.where(c == 0, theirs[1], parts[1, :, 1]))
    right.cross(0)
    coming.append(left.over_slow(odds[0]))
    left2.over_fast((0, left2.same))
    left3.over_fast((0, left3.same))
    coming += [left.over_slow(j) for j in odds[1:]]
    for earlier in coming[: len(evens)]:
        left.over_fast(earlier)
    right.segs(1)
    early = [left2.over_slow(j) for j in (*evens, *odds)]
    right.cross(1)
    right.cross(0, others=True)
    for earlier in coming[len(evens) : -1]:
        left.over_fast(earlier)
    rest = len(left.pieces)
    left.over_fast(coming[-1])
    rest += 1
    right.cross(1, others=True)
    ready = part(left, range(rest), right, [], True, 1.0, fast == 1)
    if fast > 1:
        ready = part(left, range(rest, len(left.pieces)), right, ready, True, 1.0, True)

    a, b = Right(ready[0]), Right(ready[1])
    plane = a.plane()
    a.segs(0)
    a.cross(0)
    b.plane()
    for item in early[:-1]:
        left2.over_fast(item)
    a.segs(1)
    b.segs(0)
    b.cross(0)
    a.cross(1)
    a.cross(0, others=True)
    left2.over_fast(early[-1])
    early3 = [left3.over_slow(j) for j in (*evens, *odds)]
    b.segs(1)
    a.cross(1, others=True)
    (ready_a,) = part(left2, range(len(left2.pieces)), a, [], False, 1.0, True)
    a3 = Right(ready_a)
    a3.plane()
    a3.segs(0)
    a3.cross(0)
    b.cross(0, others=True)
    b.cross(1)
    left3.over_fast(early3[0])
    b.cross(1, others=True)
    (ready_b,) = part(left2, range(len(left2.pieces)), b, [], False, 1.0, True)
    b3 = Right(ready_b)

    b3.plane()
    b3.segs(0)
    b3.cross(0)
    for item in early3[1:]:
        left3.over_fast(item)
    a3.segs(1)
    a3.cross(1)
    a3.cross(0, others=True)
    b3.segs(1)
    a3.cross(1, others=True)
    (last_a,) = part(left3, range(len(left3.pieces)), a3, [], False, factor, True)

    def home(h, value):
        slots = [i * 2 + k for i in range(rows) for k in range(2) if (i // fast) % 2 != h]
        moved = [
            send(value, ("row", "col"), [(i, partner(i // 2) * 2 + 1) for i in slots if i % 2 == k])
            for k in range(2)
        ]
        slots = [i for i in range(rows) if (i // fast) % 2 == h]
        kept = send(value, ("row", "col"), [(i * 2, i * 2 + 1) for i in slots])
        return kept, moved

    kept_a, moved_a = home(0, last_a)
    b3.cross(1)
    b3.cross(0, others=True)
    b3.cross(1, others=True)
    (last_b,) = part(left3, range(len(left3.pieces)), b3, [], False, factor, True)
    kept_b, moved_b = home(1, last_b)
    here = jnp.where(zl == 0, jnp.stack([kept_a, last_a]), jnp.stack([kept_b, last_b]))
    there = jnp.where(zl == 0, jnp.stack(moved_a), jnp.stack(moved_b))
    final = jnp.stack([jnp.where(zl == s, here, there) for s in range(2)])

    def scaled(value):
        return (value.astype(jnp.float32) * factor).astype(jnp.bfloat16)

    for item in (a, b, a3, b3):
        item.pieces = [(*p[:3], after(p[3], last_b)) for p in item.pieces]
    head = jnp.where(c == 0, slices[0].reshape(2, 2, q, w), own_block((a3, b3)))
    tail = jnp.where(c == 0, scaled(own_block((a, b))), final)
    return jnp.stack([scaled(head).reshape(height, w), tail.reshape(height, w)], axis=0)


def solution(mesh):
    spec = P("col", "seg", "row")
    fast = fast_length(mesh)

    def body(slices):
        return local(fast, slices)

    return jax.shard_map(body, mesh=mesh, in_specs=(spec,), out_specs=spec, check_vma=False)
```

```python
import functools
import math

import jax
import jax.numpy as jnp
from jax import lax
from jax.experimental import pallas as pl
from jax.experimental.pallas import tpu as pltpu
from jax.sharding import PartitionSpec as P


def fast_length(mesh):
    count = mesh.shape["row"]
    line = mesh.devices.reshape(mesh.shape["seg"], count, mesh.shape["col"])[0, :, 0]
    coords = [getattr(d, "coords", None) for d in line]
    if count < 2 or any(c is None for c in coords):
        return 1
    moving = [a for a in range(len(coords[0])) if coords[0][a] != coords[1][a]]
    if len(moving) != 1:
        return 1
    length = 1
    while length < count and all(
        coords[length][a] == coords[0][a] for a in range(len(coords[0])) if a != moving[0]
    ):
        length += 1
    return length if count % length == 0 else 1


def after(value, *others):
    return lax.optimization_barrier((value, *others))[0]


def product_kernel(n_left, n_right, by_half, earlier, scale, form, place, *refs):
    left, refs = refs[:n_left], refs[n_left:]
    right, refs = refs[:n_right], refs[n_right:]
    before, refs = refs[:earlier], refs[earlier:]
    *outs, lscr, rscr, acc, lsem, rsem, asem = refs
    halves, _, subs, cores, _, w = rscr.shape

    def right_copy(i):
        y, s, c = place[1, i], place[2, i], place[3, i]
        target = rscr.at[s, y, :, c] if by_half else rscr.at[0, y, s, c]
        return pltpu.make_async_copy(right[i], target, rsem.at[y, s, c])

    for i in range(n_right):
        pl.when(place[4, i] == 1)(right_copy(i).start)
    for i in range(n_left):
        pltpu.make_async_copy(left[i], lscr.at[i], lsem.at[i]).start()
    copies = [pltpu.make_async_copy(b, acc.at[h], asem.at[h]) for h, b in enumerate(before)]
    for copy in copies:
        copy.start()
    for copy in copies:
        copy.wait()
    if by_half:
        for i in range(n_right):
            pl.when(place[4, i] == 1)(right_copy(i).wait)
    for i in range(n_left):
        k = place[0, i]
        y, s, c = k // (subs * cores), (k // cores) % subs, k % cores
        pltpu.make_async_copy(left[i], lscr.at[i], lsem.at[i]).wait()
        if not by_half:
            pltpu.make_async_copy(right[0], rscr.at[0, y, s, c], rsem.at[y, s, c]).wait()
        for h in range(halves):
            term = jnp.dot(lscr[i], rscr[h, y, s, c], preferred_element_type=jnp.float32)
            if i or earlier:
                term += acc[h]
            if i < n_left - 1:
                acc[h] = term
            elif form == "sum":
                outs[h][...] = term
            else:
                term = (term * scale).astype(jnp.bfloat16).astype(jnp.float32)
                low, high = term[:, : w // 2], term[:, w // 2 :]
                if form == "ends":
                    low, high = jnp.where(place[5, 0] == 0, low, high), jnp.where(place[5, 0] == 0, high, low)
                if by_half:
                    for out, value in zip(outs, (low, high)):
                        out[:, h * w // 2 : (h + 1) * w // 2] = value.astype(out.dtype)
                elif form == "ends":
                    for out, value in zip(outs, (low, high)):
                        out[...] = value.astype(out.dtype)
                else:
                    outs[0][...] = term.astype(outs[0].dtype)


def product(left, right, before, by_half, scale, segs, place, form):
    q, w = left[0].shape
    n_left, n_right = len(left), len(right)
    halves = 2 if by_half else 1
    if form == "ends":
        shapes = [jax.ShapeDtypeStruct((q, w // 2), jnp.bfloat16)] * 2
    else:
        shapes = [jax.ShapeDtypeStruct((q, w), jnp.float32 if form == "sum" else jnp.bfloat16)] * halves

    def body(place_ref, *refs):
        product_kernel(n_left, n_right, by_half, len(before), scale, form, place_ref, *refs)

    return pl.pallas_call(
        body,
        out_shape=shapes,
        in_specs=[pl.BlockSpec(memory_space=pltpu.SMEM)]
        + [pl.BlockSpec(memory_space=pl.ANY)] * (n_left + n_right + len(before)),
        out_specs=[pl.BlockSpec(memory_space=pltpu.VMEM)] * len(shapes),
        scratch_shapes=[
            pltpu.VMEM((n_left, q, w), jnp.bfloat16),
            pltpu.VMEM((halves, segs, 2, 2, q, w), jnp.bfloat16),
            pltpu.VMEM((halves, q, w), jnp.float32),
            pltpu.SemaphoreType.DMA((n_left,)),
            pltpu.SemaphoreType.DMA((segs, 2, 2)),
            pltpu.SemaphoreType.DMA((halves,)),
        ],
        cost_estimate=pl.CostEstimate(
            flops=2 * halves * q * n_left * w * w, bytes_accessed=2 * n_left * w * (q + halves * w), transcendentals=0
        ),
        compiler_params=pltpu.CompilerParams(vmem_limit_bytes=40 << 20),
    )(place, *left, *right, *before)


def base_kernel(factor, place, own, *refs):
    early, late, near, far = refs[:8], refs[8:16], refs[16:20], refs[20:22]
    out, buf, sems, out_sems = refs[22:]
    half = buf.shape[-1] // 2
    c, zl = place[0], 1 - place[1]

    def gathered(pieces, slot):
        return [
            pltpu.make_async_copy(
                piece.at[:, pl.ds(pl.multiple_of(zl * half, half), half)],
                buf.at[slot, zl ^ (i // 2 % 2), c ^ (i % 2), :, pl.ds(i // 4 * half, half)],
                sems.at[i],
            )
            for i, piece in enumerate(pieces)
        ]

    def scale(slot):
        for s in range(2):
            for k in range(2):
                buf[slot, s, k] = (buf[slot, s, k].astype(jnp.float32) * factor).astype(buf.dtype)

    def run(first, second, scale_second):
        for load in first + second:
            load.start()
        stores = [pltpu.make_async_copy(buf.at[slot], out.at[slot], out_sems.at[slot]) for slot in range(2)]
        for slot, loads in enumerate((first, second)):
            for load in loads:
                load.wait()
            if slot == 0 or scale_second:
                scale(slot)
            stores[slot].start()
        for store in stores:
            store.wait()

    @pl.when(c == 0)
    def _():
        run([pltpu.make_async_copy(own, buf.at[0], sems.at[8])], gathered(early, 1), True)

    @pl.when(c == 1)
    def _():
        ends = [(zl, i % 2, i // 2, piece) for i, piece in enumerate(near)]
        ends += [(1 - zl, k, h, piece) for k, piece in enumerate(far) for h in range(2)]
        copies = [
            pltpu.make_async_copy(piece, buf.at[1, s, k, :, pl.ds(h * half, half)], sems.at[8 + i])
            for i, (s, k, h, piece) in enumerate(ends)
        ]
        run(gathered(late, 0), copies, False)


def assemble(factor, place, own, pieces):
    spec = pl.BlockSpec(memory_space=pl.ANY)
    return pl.pallas_call(
        functools.partial(base_kernel, factor),
        out_shape=jax.ShapeDtypeStruct((2, *own.shape), own.dtype),
        in_specs=[pl.BlockSpec(memory_space=pltpu.SMEM)] + [spec] * (1 + len(pieces)),
        out_specs=spec,
        scratch_shapes=[
            pltpu.VMEM((2, *own.shape), own.dtype),
            pltpu.SemaphoreType.DMA((16,)),
            pltpu.SemaphoreType.DMA((2,)),
        ],
        compiler_params=pltpu.CompilerParams(vmem_limit_bytes=24 << 20),
    )(place, own, *pieces)


def finish_kernel(place, base, first, second, out, scr, sems):
    _, half = first.shape

    @pl.when(place[0] == 1)
    def _():
        pieces = (first, second)
        loads = [pltpu.make_async_copy(p, scr.at[k], sems.at[0, k]) for k, p in enumerate(pieces)]
        stores = [
            pltpu.make_async_copy(scr.at[k], out.at[1, place[1], k, :, pl.ds(half, half)], sems.at[1, k])
            for k in range(2)
        ]
        for load in loads:
            load.start()
        for load, store in zip(loads, stores):
            load.wait()
            store.start()
        for store in stores:
            store.wait()


def finish(place, base, pieces):
    spec = pl.BlockSpec(memory_space=pl.ANY)
    return pl.pallas_call(
        finish_kernel,
        out_shape=jax.ShapeDtypeStruct(base.shape, base.dtype),
        in_specs=[pl.BlockSpec(memory_space=pltpu.SMEM)] + [spec] * 3,
        out_specs=spec,
        scratch_shapes=[pltpu.VMEM((2, *pieces[0].shape), base.dtype), pltpu.SemaphoreType.DMA((2, 2))],
        input_output_aliases={1: 0},
    )(place, base, *pieces)


def local(fast, slices):
    segs, rows, _ = (lax.axis_size(a) for a in ("seg", "row", "col"))
    slow = rows // fast
    height, w = slices.shape[1:]
    q = height // 4
    y, r, c = (lax.axis_index(a) for a in ("seg", "row", "col"))
    z, x = r // fast, r % fast
    zl = z % 2
    factor = math.sqrt(segs * height)

    def send(value, axes, pairs, gate=None):
        if gate is not None:
            value = after(value, gate)
        return lax.ppermute(value, axes, pairs)

    def along(value, dz, dx, gate=None):
        pairs = [
            (i, ((i // fast + dz) % slow) * fast + (i % fast + dx) % fast) for i in range(rows)
        ]
        return send(value, "row", pairs, gate)

    def seg_shift(value, dy, gate=None):
        return send(value, "seg", [(i, (i + dy) % segs) for i in range(segs)], gate)

    def partner(i):
        return ((i // fast) ^ 1) * fast + i % fast

    def plane_swap(value, gate=None):
        return send(value, "row", [(i, partner(i)) for i in range(rows)], gate)

    def core_swap(value):
        return send(value, "col", [(0, 1), (1, 0)])

    def row_half(block, i):
        return lax.dynamic_index_in_dim(block, i, 0, keepdims=False)

    class Left:
        def __init__(self, block):
            self.same, self.other = row_half(block, zl), row_half(block, 1 - zl)
            self.pieces = []

        def over_slow(self, j, gate=None):
            piece = along(self.same if j % 2 == 0 else self.other, j, 0, gate)
            return j, piece

        def over_fast(self, j_piece):
            j, piece = j_piece
            self.pieces.append((j, 0, piece))
            for i in range(1, fast):
                self.pieces.append((j, i, along(piece, 0, i)))

        def places(self):
            return [((z - j) % slow) * fast + (x - i) % fast for j, i, _ in self.pieces]

    class Right:
        def __init__(self, block):
            self.pieces = [(0, 0, 0, block)]

        def places(self):
            return [
                [(y - dy) % segs for dy, _, _, _ in self.pieces],
                [zl ^ s for _, s, _, _ in self.pieces],
                [c ^ k for _, _, k, _ in self.pieces],
            ]

        def add(self, key, block):
            self.pieces.append((*key, block))
            return block

        def block(self, *key):
            return [p[-1] for p in self.pieces if p[:3] == key][0]

        def plane(self, gate=None):
            return self.add((0, 1, 0), plane_swap(self.block(0, 0, 0), gate))

        def segs(self, s, gate=None):
            block = self.block(0, s, 0)
            return [self.add((dy, s, 0), seg_shift(block, dy, gate)) for dy in range(1, segs)]

        def cross(self, s, others=False):
            for dy in range(1, segs) if others else [0]:
                self.add((dy, s, 1), core_swap(self.block(dy, s, 0)))

    def part(left, chosen, right, before, by_half, scale, form):
        places = [left.places()[i] for i in chosen]
        table = [places] + right.places()
        flags = []
        for ry, rs, rc in zip(*table[1:]):
            match = lambda k: (k // 4 == ry) & (k % 2 == rc) & (by_half | (k // 2 % 2 == rs))
            flags.append(functools.reduce(jnp.logical_or, [match(k) for k in places]))
        table += [flags, [zl]]
        width = max(len(t) for t in table)
        zero = jnp.int32(0)
        place = jnp.stack(
            [jnp.stack([jnp.asarray(v, jnp.int32) for v in t] + [zero] * (width - len(t))) for t in table]
        )
        return product(
            [left.pieces[i][-1] for i in chosen],
            [p[-1] for p in right.pieces],
            before,
            by_half,
            scale,
            segs,
            place,
            form,
        )

    def own_block(halves):
        def columns(block):
            return jnp.where(zl == 0, block[:, : w // 2], block[:, w // 2 :])

        found = {
            (t, k): jnp.concatenate([columns(right.block(0, t, k)) for right in halves], axis=1)
            for t in range(2)
            for k in range(2)
        }

        def pick(s, k):
            by_core = [jnp.where(c == k, found[(t, 0)], found[(t, 1)]) for t in range(2)]
            return jnp.where(zl == s, by_core[0], by_core[1])

        return jnp.stack([jnp.stack([pick(s, k) for k in range(2)]) for s in range(2)])

    evens, odds = range(2, slow, 2), range(1, slow, 2)

    parts = slices.reshape(2, 2, 2, q, w)
    theirs = [core_swap(jnp.where(c == 0, parts[0, :, 1], parts[0, :, 0]))]
    right = Right(jnp.where(c == 0, parts[0, :, 0], theirs[0]))
    plane = right.plane()
    given = after(parts[1], right.block(0, 0, 0))
    theirs.append(core_swap(jnp.where(c == 0, given[:, 1], given[:, 0])))
    right.segs(0)
    left = Left(jnp.where(c == 0, parts[1, :, 0], theirs[1]))
    coming = [left.over_slow(j) for j in evens]
    left.over_fast((0, left.same))
    theirs = after(theirs, left.same)
    left2 = Left(jnp.where(c == 0, theirs[0], parts[0, :, 1]))
    left3 = Left(jnp.where(c == 0, theirs[1], parts[1, :, 1]))
    right.cross(0)
    coming.append(left.over_slow(odds[0]))
    left2.over_fast((0, left2.same))
    left3.over_fast((0, left3.same))
    coming += [left.over_slow(j) for j in odds[1:]]
    for earlier in coming[: len(evens)]:
        left.over_fast(earlier)
    right.segs(1)
    early = [left2.over_slow(j) for j in (*evens, *odds)]
    right.cross(1)
    right.cross(0, others=True)
    for earlier in coming[len(evens) : -1]:
        left.over_fast(earlier)
    rest = len(left.pieces)
    left.over_fast(coming[-1])
    rest += 1
    right.cross(1, others=True)
    ready = part(left, range(rest), right, [], True, 1.0, "sum" if fast > 1 else "whole")
    if fast > 1:
        ready = part(left, range(rest, len(left.pieces)), right, ready, True, 1.0, "whole")

    a, b = Right(ready[0]), Right(ready[1])
    plane = a.plane()
    a.segs(0)
    a.cross(0)
    b.plane()
    for item in early[:-1]:
        left2.over_fast(item)
    a.segs(1)
    b.segs(0)
    b.cross(0)
    a.cross(1)
    a.cross(0, others=True)
    left2.over_fast(early[-1])
    early3 = [left3.over_slow(j) for j in (*odds, *evens)]
    b.segs(1)
    a.cross(1, others=True)
    (ready_a,) = part(left2, range(len(left2.pieces)), a, [], False, 1.0, "whole")
    a3 = Right(ready_a)
    a3.plane()
    a3.segs(0)
    a3.cross(0)
    b.cross(0, others=True)
    b.cross(1)
    left3.over_fast(early3[0])
    b.cross(1, others=True)
    (ready_b,) = part(left2, range(len(left2.pieces)), b, [], False, 1.0, "whole")
    b3 = Right(ready_b)

    b3.plane()
    b3.segs(0)
    b3.cross(0)
    for item in early3[1:]:
        left3.over_fast(item)
    a3.segs(1)
    a3.cross(1)
    a3.cross(0, others=True)
    b3.segs(1)
    a3.cross(1, others=True)
    last_a = part(left3, range(len(left3.pieces)), a3, [], False, factor, "ends")

    def home(keep, away):
        moved = [send(away, ("row", "col"), [(i * 2 + k, partner(i) * 2 + 1) for i in range(rows)]) for k in range(2)]
        return [send(keep, "col", [(0, 1)]), keep], moved

    here_a, far_a = home(*last_a)
    b3.cross(1)
    b3.cross(0, others=True)
    b3.cross(1, others=True)
    last_b = part(left3, range(len(left3.pieces)), b3, [], False, factor, "ends")
    here_b, far_b = home(*last_b)
    if w % 512 == 0:
        place = jnp.stack([c, 1 - zl]).astype(jnp.int32)
        keys = [(t, k) for t in range(2) for k in range(2)]
        pieces = [right.block(0, *key) for halves in ((a, b), (a3, b3)) for right in halves for key in keys]
        base = assemble(factor, place, parts[0], [*pieces, *here_a, *here_b, *far_a])
        return finish(place, base, far_b).reshape(2, height, w)
    here = jnp.stack([jnp.concatenate([here_a[k], here_b[k]], axis=1) for k in range(2)])
    there = jnp.stack([jnp.concatenate([far_a[k], far_b[k]], axis=1) for k in range(2)])
    final = jnp.stack([jnp.where(zl == s, here, there) for s in range(2)])

    def scaled(value):
        return (value.astype(jnp.float32) * factor).astype(jnp.bfloat16)

    for item in (a, b, a3, b3):
        item.pieces = [(*p[:3], after(p[3], last_b[0])) for p in item.pieces]
    head = jnp.where(c == 0, slices[0].reshape(2, 2, q, w), own_block((a3, b3)))
    tail = jnp.where(c == 0, scaled(own_block((a, b))), final)
    return jnp.stack([scaled(head).reshape(height, w), tail.reshape(height, w)], axis=0)


def solution(mesh):
    spec = P("col", "seg", "row")
    fast = fast_length(mesh)

    def body(slices):
        return local(fast, slices)

    return jax.shard_map(body, mesh=mesh, in_specs=(spec,), out_specs=spec, check_vma=False)
```
